32 devices in a mesh: dp: 4 (over y, x), expert: 8 (over z, core).
Axes of the slice: x: 2, y: 2, z: 4, core: 2. Of those that a mesh axis runs over, the one named last changes fastest.
Arguments:
- tokens: bfloat16 [256, 4096], P('expert', 'dp'), may hold values from -6 to 6
- cotangent: bfloat16 [256, 4096], P('expert', 'dp'), may hold values from -6 to 6
- expert_ids: int32 [256, 3], P('expert'), may hold values from 0 to 5, all different within a row; in each aligned block of 32 rows (0 to 31, 32 to 63, ...) at most 16 rows name the same one
- gate_weights: float32 [256, 3], P('expert'), may hold values from 0.2 to 1
- slot_table: int32 [8], replicated, may hold values from 0 to 5, as said below
- split_count: int32 [6], replicated, may hold values from 0 to 8
- w_gate: bfloat16 [8, 4096, 768], P('expert', 'dp'), may hold values from -0.09375 to 0.09375
- w_up: bfloat16 [8, 4096, 768], P('expert', 'dp'), may hold values from -0.09375 to 0.09375
- w_down: bfloat16 [8, 768, 4096], P('expert', None, 'dp'), may hold values from -0.21875 to 0.21875
Outputs:
- mixed: bfloat16 [256, 4096], P('expert', 'dp')
- token_grad: bfloat16 [256, 4096], P('expert', 'dp')
- gate_grad: bfloat16 [8, 4096, 768], P('expert', 'dp')
- up_grad: bfloat16 [8, 4096, 768], P('expert', 'dp')
- down_grad: bfloat16 [8, 768, 4096], P('expert', None, 'dp')
The draws below stay inside these ranges and needn't reach their ends.
Inputs may be any that keep to these rules, and one draw needn't show every extreme that they name: `expert_ids`: in the rows of one device (aligned blocks of 32 rows), no expert is named more than 16 times. `slot_table`: every expert is held by one or two slots; exactly 2 experts are held by two, and those sit on slots s and s + 4 with s below 4.
All inputs are finite; a program needn't handle non-finite values.
Results may differ from the reference program's by a relative error of at most 0.028.
Values may be sent and summed in bfloat16 or wider, within the bound.
No kernel may reach another device: no remote copies, remote signals or barrier semaphores. Data moves between devices by JAX's collectives and lax.ppermute only.
A program may use at most 64 MiB of HBM per device.

```python
import math
import jax
import jax.numpy as jnp
import numpy as np
from jax import lax

D = 4096
FF = 768
TOK_DEV = 32
TOKENS = 256
SLOTS = 8
HOT = 2
EXPERTS = 6
TOP = 3
CAP = 16
N_DP = 4
N_EXPERT = 8


def draw_slot_table(key, part):
    order = jax.random.permutation(jax.random.fold_in(key, 11), EXPERTS).astype(jnp.int32)
    half_count = SLOTS // 2
    ranking = jax.random.permutation(jax.random.fold_in(key, 12), half_count)
    doubled = ranking < HOT
    cold_rank = jnp.cumsum(jnp.logical_not(doubled).astype(jnp.int32)) - 1
    second_index = jnp.where(doubled, jnp.arange(half_count, dtype=jnp.int32), half_count + cold_rank)
    second_half = order[second_index]
    return jnp.concatenate([order[:half_count], second_half]).astype(jnp.int32)


def touch_ends(drawn, stream_key, least, high):
    place = [jax.random.randint(jax.random.fold_in(stream_key, axis), (), 0, length) for axis, length in enumerate(drawn.shape)]
    widest = drawn.shape.index(max(drawn.shape))
    next_to = place[:widest] + [(place[widest] + 1) % drawn.shape[widest]] + place[widest + 1:]
    return drawn.at[tuple(place)].set(least).at[tuple(next_to)].set(high)


def level_of(own_key, extent, split, low, largest):
    gain = 1.0
    for dim, blocks in split:
        steps = jax.random.uniform(jax.random.fold_in(jax.random.fold_in(own_key, 6), dim), (blocks,), jnp.float32, low / len(split), largest / len(split))
        gain = gain * jnp.repeat(jnp.exp(steps), extent[dim] // blocks).reshape((-1,) + (1,) * (len(extent) - 1 - dim))
    return gain


def deal_out(stream_key, own, number, rows, amount, top, bound, lean):
    order = jax.random.permutation(stream_key, amount)
    heavy_load, usual = load_shares(amount, rows * top, bound, lean, True), load_shares(amount, rows * top, bound, lean, False)
    places = jnp.arange(amount)

    def named(tallies, turn):
        used = int((tallies > 0).sum())
        fixed = max(1, used // 4)
        shifted = fixed + (places - fixed + turn * (used - fixed)) % max(1, amount - fixed)
        return jnp.zeros((amount,), jnp.int32).at[order[jnp.where(places < fixed, places, shifted)]].set(jnp.asarray(tallies, jnp.int32))

    tallies = jnp.where(number % 4 == 0, named(heavy_load, number // 4), named(usual, number - number // 4 - 1))
    mixed = jax.random.permutation(jax.random.fold_in(own, 3), amount)
    giver, receiver = mixed[0:amount // 2 * 2:2], mixed[1:amount // 2 * 2:2]
    margin = jnp.minimum(tallies[giver] - 1, bound - tallies[receiver]) // 2
    margin = jnp.where((giver == order[0]) | (receiver == order[0]) | (tallies[receiver] == 0), 0, jnp.maximum(margin, 0))
    shifted = jax.random.randint(jax.random.fold_in(own, 4), (amount // 2,), 0, 1 << 20) % (margin + 1)
    tallies = tallies.at[giver].add(-shifted).at[receiver].add(shifted)
    items = jnp.searchsorted(jnp.cumsum(tallies), jnp.arange(rows * top), side="right").astype(jnp.int32)
    grid = items.reshape(top, rows).T
    grid = grid[jax.random.permutation(jax.random.fold_in(own, 1), rows)]
    turn = jax.random.randint(jax.random.fold_in(own, 2), (rows, 1), 0, top)
    return jnp.take_along_axis(grid, (jnp.arange(top)[None, :] + turn) % top, axis=1)


def load_shares(number_of, total, most, lean, full):
    weights = [(1 << 20) // math.isqrt(grade ** lean) + 1 for grade in range(1, number_of + 1)]
    largest = most if full else min(most, max(-(-total // number_of), total * weights[0] // sum(weights)))
    least = 1 if total - largest >= number_of - 1 else 0
    holding, surplus = [largest] + [least] * (number_of - 1), total - largest - least * (number_of - 1)
    while surplus > 0:
        movable = [i for i in range(1, number_of) if holding[i] < largest] or [i for i in range(1, number_of) if holding[i] < most]
        pool, remaining = sum([weights[i] for i in movable]), surplus
        for i in movable:
            addition = min(most - holding[i], max(1, remaining * weights[i] // pool), surplus)
            holding[i] = holding[i] + addition
            surplus = surplus - addition
    return np.array(holding)


def bell_draw(key, extent, width, bound, cuts=(), kind=jnp.bfloat16):
    entries = width * jax.random.normal(key, extent, jnp.float32)
    if cuts:
        entries = entries * level_of(key, extent, cuts, -0.22, 0.18)
    return jnp.clip(entries, -bound, bound).astype(kind)


def setup_inputs(seed: int = 0) -> dict:
    streams_of = jax.random.split(jax.random.key(seed), 10)
    tokens = bell_draw(streams_of[0], (TOKENS, D), 1.0, 6.0, ((0, 8), (1, 4)))
    cotangent = bell_draw(streams_of[1], (TOKENS, D), 0.5, 6.0, ((0, 8), (1, 4)))
    expert_ids_keys = jax.random.split(jax.random.fold_in(streams_of[2], 1), TOKENS // TOK_DEV)
    expert_ids_turns = jax.random.permutation(jax.random.fold_in(streams_of[2], 3), TOKENS // TOK_DEV)
    expert_ids = jax.vmap(lambda own, number: deal_out(jax.random.fold_in(streams_of[2], 2), own, number, TOK_DEV, EXPERTS, TOP, CAP, 2))(expert_ids_keys, expert_ids_turns).reshape((TOKENS, TOP))
    gate_weights = jnp.clip(0.2 + 0.8 * jax.random.uniform(streams_of[3], (TOKENS, TOP), jnp.float32) ** level_of(streams_of[3], (TOKENS, TOP), ((0, 8),), -0.2, 0.2), 0.2, 1.0)
    slot_table = draw_slot_table(jax.random.fold_in(streams_of[9], 71), 0)
    split_count = touch_ends(jax.random.randint(streams_of[5], (EXPERTS,), 0, N_EXPERT + 1), jax.random.fold_in(streams_of[5], 1), 0, N_EXPERT).astype(jnp.int32)
    w_gate = bell_draw(streams_of[6], (SLOTS, D, FF), D ** -0.5, 0.09375, ((0, 8), (1, 4)))
    w_up = bell_draw(streams_of[7], (SLOTS, D, FF), D ** -0.5, 0.09375, ((0, 8), (1, 4)))
    w_down = bell_draw(streams_of[8], (SLOTS, FF, D), FF ** -0.5, 0.21875, ((0, 8), (2, 4)))
    return {"tokens": tokens, "cotangent": cotangent, "expert_ids": expert_ids, "gate_weights": gate_weights, "slot_table": slot_table, "split_count": split_count, "w_gate": w_gate, "w_up": w_up, "w_down": w_down}


def slot_choice(expert_ids, slot_table, split_count, source):
    slot_count = slot_table.shape[0]
    expert_count = split_count.shape[0]
    slot_iota = jnp.arange(slot_count, dtype=jnp.int32)
    expert_iota = jnp.arange(expert_count, dtype=jnp.int32)
    holds = slot_table[None, :] == expert_iota[:, None]
    lower = jnp.min(jnp.where(holds, slot_iota[None, :], slot_count), axis=1)
    upper = jnp.max(jnp.where(holds, slot_iota[None, :], -1), axis=1)
    chosen = jnp.where(source < split_count, lower, upper).astype(jnp.int32)
    flat_ids = expert_ids.reshape(-1)
    matches = flat_ids[:, None] == expert_iota[None, :]
    target = jnp.sum(jnp.where(matches, chosen[None, :], 0), axis=1).astype(jnp.int32)
    onehot = (target[:, None] == slot_iota[None, :]).astype(jnp.int32)
    before = jnp.cumsum(onehot, axis=0) - onehot
    position = jnp.sum(before * onehot, axis=1).astype(jnp.int32)
    return target, position


def swiglu(gate_pre, up_pre):
    return (jax.nn.silu(gate_pre) * up_pre).astype(jnp.bfloat16)


def swiglu_back(gate_pre, up_pre, upstream):
    sigma = jax.nn.sigmoid(gate_pre)
    gate_back = upstream * up_pre * sigma * (1.0 + gate_pre * (1.0 - sigma))
    up_back = upstream * gate_pre * sigma
    return gate_back.astype(jnp.bfloat16), up_back.astype(jnp.bfloat16)


def shard_sum(left, right_mat, form):
    parts = jnp.einsum(form, left.astype(jnp.float32), right_mat.astype(jnp.float32))
    rounded = lax.optimization_barrier(parts.astype(jnp.bfloat16))
    return jnp.sum(rounded.astype(jnp.float32), axis=0)


def pair_total(grads, paired):
    partner_grads = jnp.roll(grads, SLOTS // 2, axis=0).astype(jnp.float32)
    return (grads.astype(jnp.float32) + paired[:, None, None] * partner_grads).astype(jnp.bfloat16)


def reference(tokens, cotangent, expert_ids, gate_weights, slot_table, split_count, w_gate, w_up, w_down):
    slot_rows = N_EXPERT * CAP
    shard_width = D // N_DP
    sources = jnp.arange(N_EXPERT, dtype=jnp.int32)
    grouped_ids = expert_ids.reshape(N_EXPERT, TOK_DEV, TOP)

    def place_one(group_ids, source_id):
        return slot_choice(group_ids, slot_table, split_count, source_id)

    target, position = jax.vmap(place_one)(grouped_ids, sources)
    assigned = jnp.arange(TOKENS * TOP, dtype=jnp.int32).reshape(N_EXPERT, TOK_DEV * TOP)
    source_grid = jnp.broadcast_to(sources[:, None], assigned.shape)
    layout = jnp.full((SLOTS, N_EXPERT, CAP), -1, dtype=jnp.int32)
    layout = layout.at[target, source_grid, position].set(assigned).reshape(SLOTS, slot_rows)
    gate_flat = gate_weights.reshape(-1)

    def slot_pass(carry, item):
        mixed_sum, token_sum = carry
        index, gate_mat, up_mat, down_mat = item
        valid = index >= 0
        safe = jnp.where(valid, index, 0).astype(jnp.int32)
        token = (safe // TOP).astype(jnp.int32)
        weight = jnp.where(valid, gate_flat[safe], 0.0)
        slot_in = jnp.where(valid[:, None], tokens[token], jnp.zeros((), jnp.bfloat16))
        slot_back = (weight[:, None] * cotangent[token].astype(jnp.float32)).astype(jnp.bfloat16)
        split_in = slot_in.reshape(slot_rows, N_DP, shard_width)
        gate_pre = shard_sum(split_in, gate_mat.reshape(N_DP, shard_width, FF), "rnd,ndf->nrf")
        up_pre = shard_sum(split_in, up_mat.reshape(N_DP, shard_width, FF), "rnd,ndf->nrf")
        hidden_act = swiglu(gate_pre, up_pre)
        slot_out = jnp.dot(hidden_act, down_mat, preferred_element_type=jnp.float32).astype(jnp.bfloat16)
        upstream = shard_sum(slot_back.reshape(slot_rows, N_DP, shard_width), down_mat.reshape(FF, N_DP, shard_width), "rnd,fnd->nrf")
        gate_back, up_back = swiglu_back(gate_pre, up_pre, upstream)
        grad_gate = jnp.dot(slot_in.T, gate_back, preferred_element_type=jnp.float32).astype(jnp.bfloat16)
        grad_up = jnp.dot(slot_in.T, up_back, preferred_element_type=jnp.float32).astype(jnp.bfloat16)
        grad_down = jnp.dot(hidden_act.T, slot_back, preferred_element_type=jnp.float32).astype(jnp.bfloat16)
        slot_dx = jnp.dot(gate_back, gate_mat.T, preferred_element_type=jnp.float32)
        slot_dx = (slot_dx + jnp.dot(up_back, up_mat.T, preferred_element_type=jnp.float32)).astype(jnp.bfloat16)
        mixed_sum = mixed_sum.at[token].add(weight[:, None] * slot_out.astype(jnp.float32))
        token_sum = token_sum.at[token].add(jnp.where(valid[:, None], slot_dx.astype(jnp.float32), 0.0))
        return (mixed_sum, token_sum), (grad_gate, grad_up, grad_down)

    start = (jnp.zeros((TOKENS, D), jnp.float32), jnp.zeros((TOKENS, D), jnp.float32))
    (mixed_sum, token_sum), (grad_gate, grad_up, grad_down) = lax.scan(slot_pass, start, (layout, w_gate, w_up, w_down))
    paired = (slot_table == jnp.roll(slot_table, SLOTS // 2)).astype(jnp.float32)
    return (mixed_sum.astype(jnp.bfloat16), token_sum.astype(jnp.bfloat16), pair_total(grad_gate, paired), pair_total(grad_up, paired), pair_total(grad_down, paired))
```

```python
import jax
import jax.numpy as jnp
from jax import lax
from jax.sharding import PartitionSpec as P

CORES = 2


def peer(index, step, count):
    if count & (count - 1) == 0:
        return index ^ step
    return (index + step) % count


def place_of(block, index, count):
    if count & (count - 1) == 0:
        return block ^ index
    return (block - index) % count


def to_peer(value, step):
    count = lax.axis_size("dp")
    return lax.ppermute(value, "dp", [(i, peer(i, step, count)) for i in range(count)])


def from_peer(value, step):
    count = lax.axis_size("dp")
    return lax.ppermute(value, "dp", [(peer(i, step, count), i) for i in range(count)])


def to_chip(value, step):
    count = lax.axis_size("expert")
    pairs = [(i, (i + CORES * step) % count) for i in range(count)]
    return lax.ppermute(value, "expert", pairs)


def to_sibling(value):
    count = lax.axis_size("expert")
    return lax.ppermute(value, "expert", [(i, i ^ 1) for i in range(count)])


def swiglu(gate_pre, up_pre):
    return jax.nn.silu(gate_pre) * up_pre


def swiglu_back(gate_pre, up_pre, upstream):
    sigma = jax.nn.sigmoid(gate_pre)
    gate_back = upstream * up_pre * sigma * (1.0 + gate_pre * (1.0 - sigma))
    up_back = upstream * gate_pre * sigma
    return gate_back, up_back


def dot(left, right, left_dim, right_dim):
    return lax.dot_general(
        left, right, (((left_dim,), (right_dim,)), ((), ())), preferred_element_type=jnp.float32
    )


def split_weights(weights):
    high = lax.reduce_precision(weights, 8, 7)
    middle = lax.reduce_precision(weights - high, 8, 7)
    low = weights - high - middle
    return high, middle, low


def on_device(
    tokens, cotangent, expert_ids, gate_weights, slot_table, split_count, w_gate, w_up, w_down
):
    bf16, f32 = jnp.bfloat16, jnp.float32
    slot_count = slot_table.shape[0]
    expert_count = split_count.shape[0]
    token_count, top_k = expert_ids.shape
    width = tokens.shape[1]
    hidden = w_gate.shape[2]
    capacity = max(2, (token_count * top_k + expert_count - 1) // expert_count)
    dp = lax.axis_size("dp")
    chips = slot_count // CORES
    block = -(-slot_count * capacity // dp)
    rows = block * dp
    me = lax.axis_index("expert")
    mine = lax.axis_index("dp")

    high, middle, low = split_weights(gate_weights)
    meta = jnp.concatenate([expert_ids.astype(f32), high, middle, low], axis=1).astype(bf16)
    meta = jnp.pad(meta, ((0, 0), (0, -4 * top_k % 128)))
    packet = jnp.concatenate([tokens, cotangent, meta], axis=1)
    held = jnp.stack([packet] + [to_chip(packet, step) for step in range(1, chips)])
    got = jnp.stack([held, to_sibling(held)], axis=1)
    got = got.reshape(slot_count * token_count, packet.shape[1])
    chip, core = me // CORES, me % CORES
    step_iota = jnp.arange(chips, dtype=jnp.int32)
    chip_of = (chip - step_iota) % chips
    source = chip_of[:, None] * CORES + jnp.stack([core, 1 - core])[None, :]
    source = source.reshape(-1)

    meta_all = got[:, 2 * width :].astype(f32)
    ids = meta_all[:, :top_k].astype(jnp.int32)
    weight_parts = meta_all[:, top_k : 4 * top_k].reshape(-1, 3, top_k)
    weights = weight_parts[:, 0] + weight_parts[:, 1] + weight_parts[:, 2]
    slot_iota = jnp.arange(slot_count, dtype=jnp.int32)
    expert_iota = jnp.arange(expert_count, dtype=jnp.int32)

    def rows_of(slot):
        expert = jnp.sum(jnp.where(slot_iota == slot, slot_table, 0))
        same = slot_table == expert
        lower = jnp.min(jnp.where(same, slot_iota, slot_count))
        upper = jnp.max(jnp.where(same, slot_iota, -1))
        split = jnp.sum(jnp.where(expert_iota == expert, split_count, 0))
        taken = jnp.where(source < split, lower, upper) == slot
        named = ids == expert
        weight = jnp.sum(jnp.where(named, weights, 0.0), axis=1)
        chosen = jnp.any(named, axis=1).reshape(slot_count, token_count) & taken[:, None]
        counted = chosen.astype(jnp.int32)
        position = jnp.cumsum(counted, axis=1) - counted
        row = source[:, None] * capacity + position
        row = place_of(row // block, mine, dp) * block + row % block
        return jnp.where(chosen, row, -1).reshape(-1), weight, expert

    far_slot = (me + slot_count // 2) % slot_count
    own_row, own_weight, own_expert = rows_of(me)
    far_row, far_weight, far_expert = rows_of(far_slot)
    far_row = jnp.where(own_expert == far_expert, far_row, -1)
    row_iota = jnp.arange(rows, dtype=jnp.int32)[:, None]
    own_pick = row_iota == own_row[None, :]
    far_pick = row_iota == far_row[None, :]
    pick = jnp.concatenate([own_pick, far_pick], axis=0)
    token_weight = jnp.concatenate(
        [
            jnp.sum(jnp.where(own_pick, own_weight[None, :], 0.0), axis=1),
            jnp.sum(jnp.where(far_pick, far_weight[None, :], 0.0), axis=1),
        ]
    )
    pick = pick.astype(bf16)
    both_in = dot(pick, got[:, :width], 1, 0).astype(bf16)
    both_back = dot(pick, got[:, width : 2 * width], 1, 0)
    both_back = (token_weight[:, None] * both_back).astype(bf16)
    own_in, own_back = both_in[:rows], both_back[:rows]

    gate_mat, up_mat, down_mat = w_gate[0], w_up[0], w_down[0]
    partial = jnp.concatenate(
        [
            dot(own_in, gate_mat, 1, 0).astype(bf16),
            dot(own_in, up_mat, 1, 0).astype(bf16),
            dot(own_back, down_mat, 1, 1).astype(bf16),
        ],
        axis=1,
    ).reshape(dp, block, 3 * hidden)
    total = partial[0].astype(f32)
    for step in range(1, dp):
        total = total + to_peer(partial[step], step).astype(f32)
    gate_pre, up_pre, upstream = (total[:, i * hidden : (i + 1) * hidden] for i in range(3))
    gate_back, up_back = swiglu_back(gate_pre, up_pre, upstream)
    shard = jnp.concatenate(
        [
            swiglu(gate_pre, up_pre).astype(bf16),
            gate_back.astype(bf16),
            up_back.astype(bf16),
        ],
        axis=1,
    )
    far_shard = to_chip(shard, chips // 2)
    own_all = jnp.concatenate([shard] + [from_peer(shard, step) for step in range(1, dp)])
    far_all = jnp.concatenate([far_shard] + [from_peer(far_shard, step) for step in range(1, dp)])
    hidden_act = own_all[:, :hidden]
    gate_back = own_all[:, hidden : 2 * hidden]
    up_back = own_all[:, 2 * hidden :]

    slot_out = token_weight[:rows, None] * dot(hidden_act, down_mat, 1, 0)
    slot_dx = dot(gate_back, gate_mat, 1, 1) + dot(up_back, up_mat, 1, 1)
    result = jnp.concatenate([slot_out.astype(bf16), slot_dx.astype(bf16)], axis=1)
    spread = dot(pick[:rows], result, 0, 0).astype(bf16)
    spread = spread.reshape(chips, CORES, token_count, 2 * width)
    merged = spread[:, 0].astype(f32) + to_sibling(spread[:, 1]).astype(f32)
    home = merged[0]
    for step in range(1, chips):
        home = home + to_chip(merged[chips - step].astype(bf16), step).astype(f32)
    home = home.astype(bf16)

    both = jnp.concatenate([own_all, far_all], axis=0)
    gate_grad = dot(both_in, both[:, hidden : 2 * hidden], 0, 0).astype(bf16)
    up_grad = dot(both_in, both[:, 2 * hidden :], 0, 0).astype(bf16)
    down_grad = dot(both[:, :hidden], both_back, 0, 0).astype(bf16)
    return (home[:, :width], home[:, width:], gate_grad[None], up_grad[None], down_grad[None])


def solution(mesh):
    return jax.shard_map(
        on_device,
        mesh=mesh,
        in_specs=(
            P("expert", "dp"),
            P("expert", "dp"),
            P("expert", None),
            P("expert", None),
            P(),
            P(),
            P("expert", "dp", None),
            P("expert", "dp", None),
            P("expert", None, "dp"),
        ),
        out_specs=(
            P("expert", "dp"),
            P("expert", "dp"),
            P("expert", "dp", None),
            P("expert", "dp", None),
            P("expert", None, "dp"),
        ),
        check_vma=False,
    )
```

```python
import functools

import jax
import jax.numpy as jnp
from jax import lax
from jax.experimental import pallas as pl
from jax.experimental.pallas import tpu as pltpu
from jax.sharding import PartitionSpec as P


CORES = 2
LANES = 128


def peer(index, step, count):
    if count & (count - 1) == 0:
        return index ^ step
    return (index + step) % count


def to_peer(value, step):
    count = lax.axis_size("dp")
    return lax.ppermute(value, "dp", [(i, peer(i, step, count)) for i in range(count)])


def from_peer(value, step):
    count = lax.axis_size("dp")
    return lax.ppermute(value, "dp", [(peer(i, step, count), i) for i in range(count)])


def to_chip(value, step):
    count = lax.axis_size("expert")
    pairs = [(i, (i + CORES * step) % count) for i in range(count)]
    return lax.ppermute(value, "expert", pairs)


def to_sibling(value):
    count = lax.axis_size("expert")
    return lax.ppermute(value, "expert", [(i, i ^ 1) for i in range(count)])


def dot(left, right, left_dim, right_dim):
    return lax.dot_general(
        left, right, (((left_dim,), (right_dim,)), ((), ())), preferred_element_type=jnp.float32
    )


def whole_part(value, divisor):
    return jnp.floor((value.astype(jnp.float32) + 0.5) * (1.0 / divisor)).astype(jnp.int32)


def grant(mesh_small):
    return pltpu.CompilerParams(vmem_limit_bytes=(10 if mesh_small else 48) << 20)


def pack_kernel(token_ref, id_ref, weight_ref, out_ref):
    bf16, f32 = jnp.bfloat16, jnp.float32
    width = token_ref.shape[1]
    rows, extra = out_ref.shape[0], out_ref.shape[1] - width
    out_ref[:, :width] = token_ref[...]
    weights = weight_ref[...]
    high = weights.astype(bf16).astype(f32)
    middle = (weights - high).astype(bf16).astype(f32)
    pieces = [id_ref[...].astype(f32), high, middle, weights - high - middle]
    pieces.append(jnp.zeros((extra - 4 * weights.shape[0], rows), f32))
    out_ref[:, width:] = jnp.concatenate(pieces, axis=0).T.astype(bf16)


def pack(tokens, expert_ids, gate_weights):
    rows, width = tokens.shape
    top_k = expert_ids.shape[1]
    extra = -(-4 * top_k // LANES) * LANES
    vmem = pl.BlockSpec(memory_space=pltpu.VMEM)
    return pl.pallas_call(
        pack_kernel,
        out_shape=jax.ShapeDtypeStruct((rows, width + extra), jnp.bfloat16),
        in_specs=[vmem] * 3,
        out_specs=vmem,
        compiler_params=grant(True),
    )(tokens, expert_ids.T, gate_weights.T)


def joined(refs):
    return jnp.concatenate([ref[...] for ref in refs], axis=0)


def route_kernel(sizes, table_ref, split_ref, *refs):
    token_count, top_k, width, capacity, block, dp, chips = sizes
    data_refs, (pick_ref, scale_ref, all_ref, own_ref) = refs[:-4], refs[-4:]
    bf16, f32 = jnp.bfloat16, jnp.float32
    slot_count = chips * CORES
    half = chips * token_count
    rows = block * dp
    me = lax.axis_index("expert")
    mine = lax.axis_index("dp")
    partner = lax.rem(me + slot_count // 2, slot_count)
    expert = table_ref[me]
    paired = (expert == table_ref[partner]).astype(jnp.int32)
    split = split_ref[expert]
    lower = (me < slot_count // 2).astype(jnp.int32)
    chip, core = me // CORES, lax.rem(me, CORES)

    count = CORES * half
    data = joined(data_refs)
    meta = data[:, width:].astype(f32)
    named = jnp.zeros((count, 1), jnp.bool_)
    pieces = [jnp.zeros((count, 1), f32) for _ in range(3)]
    for k in range(top_k):
        hit = meta[:, k : k + 1] == expert.astype(f32)
        named = named | hit
        for i in range(3):
            first = top_k * (i + 1) + k
            pieces[i] = pieces[i] + jnp.where(hit, meta[:, first : first + 1], 0.0)
    token = lax.broadcasted_iota(jnp.int32, (count, 1), 0)
    part = (token >= half).astype(jnp.int32)
    chip_of = chip - whole_part(token - part * half, token_count)
    chip_of = jnp.where(chip_of < 0, chip_of + chips, chip_of)
    source = chip_of * CORES + jnp.where(part == 0, core, 1 - core)
    in_lower = (source < split).astype(jnp.int32)
    taken = (paired == 0) | (in_lower == lower)
    at = lax.broadcasted_iota(jnp.int32, (half, half), 0)
    before = lax.broadcasted_iota(jnp.int32, (half, half), 1)
    same = whole_part(at, token_count) == whole_part(before, token_count)
    earlier = jnp.where(same & (before < at), 1.0, 0.0).astype(bf16)
    counted = jnp.broadcast_to(jnp.where(named, 1.0, 0.0), (count, LANES)).astype(bf16)
    position = jnp.concatenate(
        [dot(earlier, counted[:half], 1, 0), dot(earlier, counted[half:], 1, 0)], axis=0
    )[:, :1].astype(jnp.int32)
    row = source * capacity + position
    row_block = whole_part(row, block)
    if dp & (dp - 1) == 0:
        place = row_block ^ mine
    else:
        place = row_block - mine
        place = jnp.where(place < 0, place + dp, place)
    row = jnp.where(named, (place - row_block) * block + row, -1)
    row_lane = lax.broadcasted_iota(jnp.int32, (count, rows), 1)
    pick = jnp.where(row_lane == row, 1.0, 0.0).T.astype(bf16)
    pick_ref[...] = pick
    lane = lax.broadcasted_iota(jnp.int32, (count, LANES), 1)
    facts = jnp.where(lane == 3, jnp.where(taken, 1.0, 0.0), 0.0)
    for i in range(3):
        facts = jnp.where(lane == i, pieces[i], facts)
    scale = dot(pick, facts.astype(bf16), 1, 0)
    gathered = dot(pick, data[:, :width], 1, 0)
    own = scale[:, 3:4]
    weight = scale[:, 0:1] + scale[:, 1:2] + scale[:, 2:3]
    column = lax.broadcasted_iota(jnp.int32, (rows, LANES), 1)
    scale_ref[...] = jnp.where(
        column == 0, weight, jnp.where(column == 1, weight * own, paired.astype(f32))
    )
    all_ref[...] = gathered.astype(bf16)
    own_ref[...] = (gathered * own).astype(bf16)


def route(slot_table, split_count, packets, sizes):
    token_count, _, width, _, block, dp, chips = sizes
    rows, half = block * dp, chips * token_count
    smem = pl.BlockSpec(memory_space=pltpu.SMEM)
    vmem = pl.BlockSpec(memory_space=pltpu.VMEM)
    return pl.pallas_call(
        functools.partial(route_kernel, sizes),
        out_shape=(
            jax.ShapeDtypeStruct((rows, CORES * half), jnp.bfloat16),
            jax.ShapeDtypeStruct((rows, LANES), jnp.float32),
            jax.ShapeDtypeStruct((rows, width), jnp.bfloat16),
            jax.ShapeDtypeStruct((rows, width), jnp.bfloat16),
        ),
        in_specs=[smem, smem] + [vmem] * len(packets),
        out_specs=(vmem, vmem, vmem, vmem),
        compiler_params=grant(chips <= 4),
        cost_estimate=pl.CostEstimate(
            flops=4 * rows * half * width, bytes_accessed=8 * half * width, transcendentals=0
        ),
    )(slot_table, split_count, *packets)


def back_kernel(pick_ref, scale_ref, *refs):
    data_refs, (all_ref, own_ref) = refs[:-2], refs[-2:]
    back = dot(pick_ref[...], joined(data_refs), 1, 0)
    all_ref[...] = (scale_ref[:, 0:1] * back).astype(jnp.bfloat16)
    own_ref[...] = (scale_ref[:, 1:2] * back).astype(jnp.bfloat16)


def backward_rows(pick, scale, cots):
    rows, width = pick.shape[0], cots[0].shape[-1]
    vmem = pl.BlockSpec(memory_space=pltpu.VMEM)
    shape = jax.ShapeDtypeStruct((rows, width), jnp.bfloat16)
    return pl.pallas_call(
        back_kernel,
        out_shape=(shape, shape),
        in_specs=[vmem] * (2 + len(cots)),
        out_specs=(vmem, vmem),
        compiler_params=grant(len(cots) > 2),
        cost_estimate=pl.CostEstimate(
            flops=2 * rows * pick.shape[1] * width,
            bytes_accessed=2 * pick.shape[1] * width,
            transcendentals=0,
        ),
    )(pick, scale, *cots)


def gathered(value, chips):
    blocks = [value]
    for step in range(1, chips):
        blocks.append(to_chip(value, step))
    if chips > 4:
        blocks = [jnp.concatenate(blocks)]
    others = []
    for item in blocks:
        others.append(to_sibling(item))
    return blocks + others


def on_device(
    tokens, cotangent, expert_ids, gate_weights, slot_table, split_count, w_gate, w_up, w_down
):
    bf16, f32 = jnp.bfloat16, jnp.float32
    slot_count = slot_table.shape[0]
    expert_count = split_count.shape[0]
    token_count, top_k = expert_ids.shape
    width = tokens.shape[1]
    hidden = w_gate.shape[2]
    capacity = max(2, (token_count * top_k + expert_count - 1) // expert_count)
    dp = lax.axis_size("dp")
    chips = slot_count // CORES
    block = -(-slot_count * capacity // dp)
    sizes = (token_count, top_k, width, capacity, block, dp, chips)

    packets = gathered(pack(tokens, expert_ids, gate_weights), chips)
    cots = gathered(cotangent, chips)
    pick, scale, rows_all, rows_own = route(slot_table, split_count, packets, sizes)

    gate_mat, up_mat, down_mat = w_gate[0], w_up[0], w_down[0]
    partial = [dot(rows_own, gate_mat, 1, 0).astype(bf16), dot(rows_own, up_mat, 1, 0).astype(bf16)]
    gate_up = reduced(jnp.concatenate(partial, axis=1), dp)
    back_all, back_own = backward_rows(pick, scale, cots)
    upstream = reduced(dot(back_own, down_mat, 1, 1).astype(bf16), dp)
    gate_pre, up_pre = gate_up[:, :hidden], gate_up[:, hidden:]
    sigma = jax.nn.sigmoid(gate_pre)
    hidden_act = gate_pre * sigma * up_pre
    gate_back = upstream * up_pre * sigma * (1.0 + gate_pre * (1.0 - sigma))
    up_back = upstream * gate_pre * sigma
    shard = jnp.concatenate([hidden_act, gate_back, up_back], axis=1).astype(bf16)
    own = spread_out(shard, dp)
    far_shard = to_chip(shard, chips // 2)

    slot_out = scale[:, 1:2] * dot(own[:, :hidden], down_mat, 1, 0)
    slot_dx = dot(own[:, hidden : 2 * hidden], gate_mat, 1, 1)
    slot_dx = slot_dx + dot(own[:, 2 * hidden :], up_mat, 1, 1)
    result = jnp.concatenate([slot_out.astype(bf16), slot_dx.astype(bf16)], axis=1)
    home = dot(pick, result, 0, 0).astype(bf16)
    home = home.reshape(CORES, chips, token_count, 2 * width)
    other = to_sibling(home[1])
    home = home[0].astype(f32) + other.astype(f32)
    total = home[0]
    for step in range(1, chips):
        total = total + to_chip(home[chips - step].astype(bf16), step).astype(f32)
    total = total.astype(bf16)

    shard = shard + scale[:block, 2:3].astype(bf16) * far_shard
    merged = spread_out(shard, dp)
    gate_grad = dot(rows_all, merged[:, hidden : 2 * hidden], 0, 0).astype(bf16)
    up_grad = dot(rows_all, merged[:, 2 * hidden :], 0, 0).astype(bf16)
    down_grad = dot(merged[:, :hidden], back_all, 0, 0).astype(bf16)
    return (total[:, :width], total[:, width:], gate_grad[None], up_grad[None], down_grad[None])


def reduced(partial, count):
    blocks = partial.reshape(count, -1, partial.shape[1])
    total = blocks[0].astype(jnp.float32)
    for step in range(1, count):
        total = total + to_peer(blocks[step], step).astype(jnp.float32)
    return total


def spread_out(value, count):
    blocks = [value]
    for step in range(1, count):
        blocks.append(from_peer(value, step))
    return jnp.concatenate(blocks)


def solution(mesh):
    return jax.shard_map(
        on_device,
        mesh=mesh,
        in_specs=(
            P("expert", "dp"),
            P("expert", "dp"),
            P("expert", None),
            P("expert", None),
            P(),
            P(),
            P("expert", "dp", None),
            P("expert", "dp", None),
            P("expert", None, "dp"),
        ),
        out_specs=(
            P("expert", "dp"),
            P("expert", "dp"),
            P("expert", "dp", None),
            P("expert", "dp", None),
            P("expert", None, "dp"),
        ),
        check_vma=False,
    )
```
